32 devices in a mesh: wide: 8 (over z, y), tp: 4 (over x, core).
Axes of the slice: x: 2, y: 2, z: 4, core: 2. Of those that a mesh axis runs over, the one named last changes fastest.
Arguments:
- stream: bfloat16 [4096, 768], P(('wide', 'tp')), may hold values from -6 to 6
- segment_ids: int32 [4096], P('wide'), may hold values from 0 to 4, as said below
- cotangent: bfloat16 [4096, 768], P(('wide', 'tp')), may hold values from -6 to 6
- norm_gain: bfloat16 [2, 768], P(None, 'wide'), may hold values from 0.5 to 1.5
- in_weight: bfloat16 [2, 768, 2, 1536], P(None, 'wide', None, 'tp'), may hold values from -0.21875 to 0.21875
- bc_weight: bfloat16 [2, 768, 256], P(None, 'wide'), may hold values from -0.21875 to 0.21875
- step_weight: bfloat16 [2, 768, 24], P(None, 'wide', 'tp'), may hold values from -0.21875 to 0.21875
- filter_x: bfloat16 [2, 5, 24, 64], P(None, None, 'tp', 'wide'), may hold values from -3 to 3
- filter_bc: bfloat16 [2, 5, 256], P(None, None, 'wide'), may hold values from -3 to 3
- decay_log: float32 [2, 24], P(None, 'tp'), may hold values from -4 to 1
- step_bias: float32 [2, 24], P(None, 'tp'), may hold values from -6 to -3
- skip_gain: float32 [2, 24], P(None, 'tp'), may hold values from 0.5 to 1.5
- gate_gain: bfloat16 [2, 24, 64], P(None, 'tp', 'wide'), may hold values from 0.5 to 1.5
- out_weight: bfloat16 [2, 1536, 768], P(None, 'tp', 'wide'), may hold values from -0.15625 to 0.15625
Outputs:
- result: float32 [4096, 768], P(('wide', 'tp'))
- stream_grad: float32 [4096, 768], P(('wide', 'tp'))
- norm_gain_grad: float32 [2, 768], P(None, ('wide', 'tp'))
- in_weight_grad: float32 [2, 768, 2, 1536], P(None, 'wide', None, 'tp')
- bc_weight_grad: float32 [2, 768, 256], P(None, ('wide', 'tp'))
- step_weight_grad: float32 [2, 768, 24], P(None, 'wide', 'tp')
- filter_x_grad: float32 [2, 5, 24, 64], P(None, None, 'tp', 'wide')
- filter_bc_grad: float32 [2, 5, 256], P(None, None, ('wide', 'tp'))
- decay_log_grad: float32 [2, 24], P(None, 'tp')
- step_bias_grad: float32 [2, 24], P(None, 'tp')
- skip_gain_grad: float32 [2, 24], P(None, 'tp')
- gate_gain_grad: float32 [2, 24, 64], P(None, 'tp', 'wide')
- out_weight_grad: float32 [2, 1536, 768], P(None, 'tp', 'wide')
The draws below stay inside these ranges and needn't reach their ends.
Inputs may be any that keep to these rules, and one draw needn't show every extreme that they name: segment_ids[t] = (t + o) // 1024 for one offset o with 1 <= o < 1024, the same for the whole stream: the numbers never fall, and every segment but the first and the last has exactly 1024 tokens.
All inputs are finite; a program needn't handle non-finite values.
Results may differ from the reference program's by a relative error of at most 0.025.
Values may be sent and summed in bfloat16 or wider, within the bound.
No kernel may reach another device: no remote copies, remote signals or barrier semaphores. Data moves between devices by JAX's collectives and lax.ppermute only.
A program may use at most 256 MiB of HBM per device.

```python
from functools import partial
import jax
import jax.numpy as jnp
from jax import lax

D = 768
HEADS = 24
HEADDIM = 64
STATE = 128
KCONV = 4
SPAN = 128
SEQ = 1024
LAYERS = 2
INNER = 1536
TOKENS = 4096
N_TP = 4


def draw_segment_ids(key, part):
    offset = jax.random.randint(key, (), 1, SEQ, dtype=jnp.int32)
    positions = jnp.arange(TOKENS, dtype=jnp.int32)
    return (positions + offset) // SEQ


def shard_levels(stream_key, extent, cuts, low, largest):
    def one(dim, shards_of):
        draws = jax.random.uniform(jax.random.fold_in(jax.random.fold_in(stream_key, 6), dim), (shards_of,), jnp.float32, low / len(cuts), largest / len(cuts))
        return jnp.repeat(jnp.exp(draws), extent[dim] // shards_of).reshape((-1,) + (1,) * (len(extent) - dim - 1))

    loudness = one(*cuts[0])
    for cut in cuts[1:]:
        loudness = loudness * one(*cut)
    return loudness


def centred(stream_key, dims, spread, bound, cuts=(), kind=jnp.bfloat16):
    level = shard_levels(stream_key, dims, cuts, -0.22, 0.18) if cuts else 1.0
    values = jax.random.normal(stream_key, dims, jnp.float32) * spread * level
    return jnp.minimum(jnp.maximum(values, -bound), bound).astype(kind)


def setup_inputs(seed: int = 0) -> dict:
    seeds = jax.random.split(jax.random.key(seed), 15)
    return {
        "stream": centred(seeds[0], (TOKENS, D), 1.0, 6.0, ((0, 32),)),
        "segment_ids": draw_segment_ids(jax.random.fold_in(seeds[14], 71), 0),
        "cotangent": centred(seeds[2], (TOKENS, D), 1.0, 6.0, ((0, 32),)),
        "norm_gain": jnp.clip(1.0 + 0.1 * jax.random.normal(seeds[3], (LAYERS, D), jnp.float32), 0.5, 1.5).astype(jnp.bfloat16),
        "in_weight": centred(seeds[4], (LAYERS, D, 2, INNER), D ** -0.5, 0.21875, ((1, 8), (3, 4))),
        "bc_weight": centred(seeds[5], (LAYERS, D, 2 * STATE), D ** -0.5, 0.21875, ((1, 8),)),
        "step_weight": centred(seeds[6], (LAYERS, D, HEADS), D ** -0.5, 0.21875, ((1, 8), (2, 4))),
        "filter_x": centred(seeds[7], (LAYERS, KCONV + 1, HEADS, HEADDIM), 0.5, 3.0, ((2, 4), (3, 8))),
        "filter_bc": centred(seeds[8], (LAYERS, KCONV + 1, 2 * STATE), 0.5, 3.0, ((2, 8),)),
        "decay_log": jnp.clip(-4.0 + 5.0 * jax.random.uniform(seeds[9], (LAYERS, HEADS), jnp.float32) ** shard_levels(seeds[9], (LAYERS, HEADS), ((1, 4),), -0.2, 0.2), -4.0, 1.0),
        "step_bias": jnp.clip(-6.0 + 3.0 * jax.random.uniform(seeds[10], (LAYERS, HEADS), jnp.float32) ** shard_levels(seeds[10], (LAYERS, HEADS), ((1, 4),), -0.2, 0.2), -6.0, -3.0),
        "skip_gain": jnp.clip(0.5 + 1.0 * jax.random.uniform(seeds[11], (LAYERS, HEADS), jnp.float32) ** shard_levels(seeds[11], (LAYERS, HEADS), ((1, 4),), -0.2, 0.2), 0.5, 1.5),
        "gate_gain": jnp.clip(1.0 + 0.1 * jax.random.normal(seeds[12], (LAYERS, HEADS, HEADDIM), jnp.float32), 0.5, 1.5).astype(jnp.bfloat16),
        "out_weight": centred(seeds[13], (LAYERS, INNER, D), INNER ** -0.5, 0.15625, ((1, 4), (2, 8))),
    }


EPS = 1e-05
HIGHEST = lax.Precision.HIGHEST

def silu_slope(value):
    sigma = jax.nn.sigmoid(value)
    return sigma * (1.0 + value * (1.0 - sigma))

def inner_rows(left, right):
    return lax.dot_general(left, right, (((0,), (0,)), ((), ())), preferred_element_type=jnp.float32)

def outer_cols(left, right):
    return lax.dot_general(left, right, (((1,), (1,)), ((), ())), preferred_element_type=jnp.float32)

def conv_apply(padded, seg_pad, filters):
    taps = filters.shape[0] - 1
    length = padded.shape[0] - taps + 1
    seg_now = seg_pad[taps - 1:]
    total = jnp.broadcast_to(filters[taps][None, :], (length, padded.shape[1]))
    for offset in range(taps):
        keep = (seg_pad[offset:offset + length] == seg_now).astype(jnp.float32)
        total = total + filters[offset][None, :] * padded[offset:offset + length] * keep[:, None]
    return total

def block_tail(block_values, input_block, block_steps, block_seg, prev_seg, rates):
    length = block_seg.shape[0]
    logs = jnp.cumsum(block_steps * rates[None, :], axis=0).T
    last_seg = block_seg[length - 1]
    same_last = (block_seg == last_seg).astype(jnp.float32)
    tail = jnp.exp(logs[:, length - 1:] - logs).T * block_steps * same_last[:, None]
    local = jnp.einsum('sh,shp,sn->hpn', tail, block_values, input_block, precision=HIGHEST)
    through = jnp.exp(logs[:, length - 1]) * (last_seg == prev_seg).astype(jnp.float32)
    return (logs, local, through)

def block_step(rates, skips, state, pieces):
    block_values, input_block, output_block, block_steps, block_seg, prev_seg = pieces
    length = block_seg.shape[0]
    logs, local, through = block_tail(block_values, input_block, block_steps, block_seg, prev_seg, rates)
    rowids = lax.broadcasted_iota(jnp.int32, (length, length), 0)
    colids = lax.broadcasted_iota(jnp.int32, (length, length), 1)
    allowed = (rowids >= colids) & (block_seg[:, None] == block_seg[None, :])
    gaps = jnp.where(allowed[None], logs[:, :, None] - logs[:, None, :], 0.0)
    decays = jnp.where(allowed[None], jnp.exp(gaps), 0.0)
    scores = jnp.dot(output_block, input_block.T, precision=HIGHEST)
    mixing = decays * scores[None] * block_steps.T[:, None, :]
    inner = jnp.einsum('hts,shp->thp', mixing, block_values, precision=HIGHEST)
    first = (block_seg == prev_seg).astype(jnp.float32)
    carry_in = jnp.exp(logs).T * first[:, None]
    from_state = jnp.einsum('tn,hpn->thp', output_block, state, precision=HIGHEST) * carry_in[:, :, None]
    outputs = inner + from_state + skips[None, :, None] * block_values
    return (through[:, None, None] * state + local, outputs)

def ssd_chain(values, input_mat, output_mat, steps, rates, skips, state_in, segs, seg_before):
    step_fn = jax.checkpoint(partial(block_step, rates, skips))
    final, outputs = lax.scan(step_fn, state_in, (values, input_mat, output_mat, steps, segs, seg_before))
    return (outputs, final)

def group_chain(state_in, segs, seg_before, values, input_mat, output_mat, steps, rates, skips):
    return ssd_chain(values, input_mat, output_mat, steps, rates, skips, state_in, segs, seg_before)[0]

def reference(stream, segment_ids, cotangent, norm_gain, in_weight, bc_weight, step_weight, filter_x, filter_bc, decay_log, step_bias, skip_gain, gate_gain, out_weight):
    group_heads = HEADS // N_TP
    blocks = TOKENS // SPAN
    margin = KCONV - 1
    seg_pad = jnp.concatenate([jnp.zeros((margin,), jnp.int32), segment_ids.astype(jnp.int32)])
    segs = segment_ids.reshape(blocks, SPAN)
    seg_before = jnp.concatenate([seg_pad[margin - 1:margin], segment_ids[SPAN - 1:TOKENS - 1:SPAN]])
    zero_state = jnp.zeros((group_heads, HEADDIM, STATE), jnp.float32)
    hidden = stream.astype(jnp.float32)
    memos = []
    for layer in range(LAYERS):
        scale_in = lax.rsqrt(lax.optimization_barrier(jnp.mean(hidden * hidden, axis=-1, keepdims=True)) + EPS)
        gain_in = norm_gain[layer].astype(jnp.float32)
        normed = (hidden * scale_in * gain_in[None, :]).astype(jnp.bfloat16)
        weight_zx = in_weight[layer].reshape(D, 2 * INNER)
        proj_zx = jnp.dot(normed, weight_zx, preferred_element_type=jnp.float32).astype(jnp.bfloat16)
        gate_in = proj_zx[:, :INNER]
        inputs_x = proj_zx[:, INNER:]
        inputs_bc = jnp.dot(normed, bc_weight[layer], preferred_element_type=jnp.float32).astype(jnp.bfloat16)
        step_raw = jnp.dot(normed, step_weight[layer], preferred_element_type=jnp.float32)
        filters_x = filter_x[layer].astype(jnp.float32).reshape(KCONV + 1, INNER)
        filters_bc = filter_bc[layer].astype(jnp.float32)
        padded_x = jnp.concatenate([jnp.zeros((margin, INNER), jnp.float32), inputs_x.astype(jnp.float32)])
        padded_bc = jnp.concatenate([jnp.zeros((margin, 2 * STATE), jnp.float32), inputs_bc.astype(jnp.float32)])
        pre_x = conv_apply(padded_x, seg_pad, filters_x)
        pre_bc = conv_apply(padded_bc, seg_pad, filters_bc)
        act_x = jax.nn.silu(pre_x)
        act_bc = jax.nn.silu(pre_bc)
        rates = -jnp.exp(decay_log[layer])
        steps = jax.nn.softplus(step_raw + step_bias[layer][None, :])
        input_mat = act_bc[:, :STATE].reshape(blocks, SPAN, STATE)
        output_mat = act_bc[:, STATE:].reshape(blocks, SPAN, STATE)
        values = act_x.reshape(blocks, SPAN, HEADS, HEADDIM)
        step_blocks = steps.reshape(blocks, SPAN, HEADS)
        outputs_all = []
        pullbacks = []
        for group in range(N_TP):
            lower = group * group_heads
            upper = lower + group_heads
            outputs, pullback = jax.vjp(partial(group_chain, zero_state, segs, seg_before), values[:, :, lower:upper], input_mat, output_mat, step_blocks[:, :, lower:upper], rates[lower:upper], skip_gain[layer][lower:upper])
            outputs_all.append(outputs)
            pullbacks.append(pullback)
        y_all = jnp.concatenate(outputs_all, axis=2).reshape(TOKENS, INNER)
        gate_act = jax.nn.silu(gate_in.astype(jnp.float32))
        mixed = y_all * gate_act
        scale_gate = lax.rsqrt(lax.optimization_barrier(jnp.sum(mixed * mixed, axis=-1, keepdims=True)) / INNER + EPS)
        gains_gate = gate_gain[layer].astype(jnp.float32).reshape(INNER)
        gated = (mixed * scale_gate * gains_gate[None, :]).astype(jnp.bfloat16)
        memos.append((hidden, scale_in, gain_in, normed, weight_zx, gate_in, step_raw, padded_x, padded_bc, filters_x, filters_bc, pre_x, pre_bc, rates, pullbacks, y_all, gate_act, mixed, scale_gate, gains_gate, gated))
        hidden = hidden + jnp.dot(gated, out_weight[layer], preferred_element_type=jnp.float32)
    result = hidden
    grad = cotangent.astype(jnp.float32)
    lists = [[None] * LAYERS for index in range(11)]
    for layer in reversed(range(LAYERS)):
        hidden_old, scale_in, gain_in, normed, weight_zx, gate_in, step_raw, padded_x, padded_bc, filters_x, filters_bc, pre_x, pre_bc, rates, pullbacks, y_all, gate_act, mixed, scale_gate, gains_gate, gated = memos[layer]
        grad_b = grad.astype(jnp.bfloat16)
        out_grad = inner_rows(gated, grad_b)
        grad_gated = outer_cols(grad_b, out_weight[layer])
        gate_grad = lax.optimization_barrier(jnp.sum(grad_gated * mixed * scale_gate, axis=0)).reshape(HEADS, HEADDIM)
        weighted = grad_gated * gains_gate[None, :]
        grad_mixed = scale_gate * weighted - mixed * scale_gate ** 3 * lax.optimization_barrier(jnp.sum(weighted * mixed, axis=-1, keepdims=True)) / INNER
        grad_y = (grad_mixed * gate_act).reshape(blocks, SPAN, HEADS, HEADDIM)
        grad_gate = grad_mixed * y_all * silu_slope(gate_in.astype(jnp.float32))
        group_heads = HEADS // N_TP
        parts_x, parts_steps, parts_rates, parts_skips, shares_b = ([], [], [], [], [])
        for group in range(N_TP):
            lower = group * group_heads
            upper = lower + group_heads
            grad_values, grad_input, grad_output, grad_steps, grad_rates, grad_skips = pullbacks[group](grad_y[:, :, lower:upper])
            parts_x.append(grad_values)
            parts_steps.append(grad_steps)
            parts_rates.append(grad_rates)
            parts_skips.append(grad_skips)
            shares_b.append(jnp.concatenate([grad_input.reshape(TOKENS, STATE), grad_output.reshape(TOKENS, STATE)], axis=1))
        grad_act_x = jnp.concatenate(parts_x, axis=2).reshape(TOKENS, INNER)
        grad_steps_all = jnp.concatenate(parts_steps, axis=2).reshape(TOKENS, HEADS)
        decay_grad = jnp.concatenate(parts_rates) * rates
        skip_grad = jnp.concatenate(parts_skips)
        grad_step_raw = grad_steps_all * jax.nn.sigmoid(step_raw + step_bias[layer][None, :])
        bias_grad = lax.optimization_barrier(jnp.sum(grad_step_raw, axis=0))
        conv_x_pull = jax.vjp(lambda rowset, filt: conv_apply(rowset, seg_pad, filt), padded_x, filters_x)[1]
        conv_bc_pull = jax.vjp(lambda rowset, filt: conv_apply(rowset, seg_pad, filt), padded_bc, filters_bc)[1]
        grad_pad_x, filt_x_grad = conv_x_pull(grad_act_x * silu_slope(pre_x))
        grad_zx = jnp.concatenate([grad_gate, grad_pad_x[margin:]], axis=1).astype(jnp.bfloat16)
        grad_step_b = grad_step_raw.astype(jnp.bfloat16)
        filt_bc_grad = jnp.zeros_like(filters_bc)
        bc_grad = jnp.zeros((D, 2 * STATE), jnp.float32)
        grad_normed = outer_cols(grad_zx, weight_zx) + outer_cols(grad_step_b, step_weight[layer])
        for group in range(N_TP):
            grad_pad_bc, group_filt = conv_bc_pull(shares_b[group] * silu_slope(pre_bc))
            filt_bc_grad = filt_bc_grad + group_filt
            share = grad_pad_bc[margin:].astype(jnp.bfloat16)
            bc_grad = bc_grad + inner_rows(normed, share)
            grad_normed = grad_normed + outer_cols(share, bc_weight[layer])
        in_grad = inner_rows(normed, grad_zx).reshape(D, 2, INNER)
        step_grad = inner_rows(normed, grad_step_b)
        gain_grad = lax.optimization_barrier(jnp.sum(grad_normed * hidden_old * scale_in, axis=0))
        weighted_in = grad_normed * gain_in[None, :]
        grad = grad + scale_in * weighted_in - hidden_old * scale_in ** 3 * lax.optimization_barrier(jnp.mean(weighted_in * hidden_old, axis=-1, keepdims=True))
        found = (gain_grad, in_grad, bc_grad, step_grad, filt_x_grad.reshape(KCONV + 1, HEADS, HEADDIM), filt_bc_grad, decay_grad, bias_grad, skip_grad, gate_grad, out_grad)
        for index in range(11):
            lists[index][layer] = found[index]
    stacked = [jnp.stack(entries, axis=0) for entries in lists]
    return (result, grad, stacked[0], stacked[1], stacked[2], stacked[3], stacked[4], stacked[5], stacked[6], stacked[7], stacked[8], stacked[9], stacked[10])
```

```python
from functools import partial

import jax
import jax.numpy as jnp
from jax import lax
from jax.experimental import pallas as pl
from jax.experimental.pallas import tpu as pltpu
from jax.sharding import PartitionSpec as P

D = 768
HEADDIM = 64
STATE = 128
KCONV = 4
SEQ = 1024
LAYERS = 2
INNER = 1536
EPS = 1e-05
OFF = 256.0
T = 128
HIGHEST = lax.Precision.HIGHEST
F32 = jnp.float32
BF16 = jnp.bfloat16


def mm(a, b):
    return lax.dot_general(a, b, (((1,), (0,)), ((), ())), preferred_element_type=F32)


def mm_nt(a, b):
    return lax.dot_general(a, b, (((1,), (1,)), ((), ())), preferred_element_type=F32)


def mm_tn(a, b):
    return lax.dot_general(a, b, (((0,), (0,)), ((), ())), preferred_element_type=F32)


def call(body, outs, *args, scratch=(), smem=0):
    vm = pl.BlockSpec(memory_space=pltpu.VMEM)
    sm = pl.BlockSpec(memory_space=pltpu.SMEM)
    specs = [sm] * smem + [vm] * (len(args) - smem)
    return pl.pallas_call(
        body,
        out_shape=[jax.ShapeDtypeStruct(s, d) for s, d in outs],
        in_specs=specs,
        out_specs=[vm] * len(outs),
        scratch_shapes=[pltpu.VMEM(s, d) for s, d in scratch],
        compiler_params=pltpu.CompilerParams(vmem_limit_bytes=56 * 1024 * 1024),
    )(*args)


def sigmoid(v):
    return 1.0 / (1.0 + jnp.exp(-v))


def low_lanes():
    return lax.broadcasted_iota(jnp.int32, (T, 2 * HEADDIM), 1) < HEADDIM


def spread(cols, base, heads):
    low = low_lanes()
    parts = []
    for q in range(heads // 2):
        a = cols[:, base + 2 * q : base + 2 * q + 1]
        b = cols[:, base + 2 * q + 1 : base + 2 * q + 2]
        parts.append(jnp.where(low, a, b))
    return jnp.concatenate(parts, axis=1)


def to_cols(rows):
    pad = jnp.zeros((128 - rows.shape[0], rows.shape[1]), F32)
    return jnp.transpose(jnp.concatenate([rows, pad], axis=0))


def state_rows(message, heads, side):
    top = heads * HEADDIM
    factor = message[top : top + 8, :].astype(F32) + message[top + 8 : top + 16, :].astype(F32)
    if not side:
        return message[:top, :].astype(F32)
    return jnp.concatenate(
        [jnp.broadcast_to(factor[h : h + 1, :], (HEADDIM, STATE)) for h in range(heads)], axis=0
    )


def joined(messages, heads):
    total = state_rows(messages[-1], heads, False)
    for message in messages[-2::-1]:
        total = state_rows(message, heads, False) + state_rows(message, heads, True) * total
    return total


def pack_message(ref, state, through, top):
    ref[:top, :] = state.astype(BF16)
    wide = jnp.broadcast_to(through, (8, STATE))
    high = wide.astype(BF16)
    ref[top:, :] = jnp.concatenate([high.astype(F32), wide - high.astype(F32)], axis=0).astype(BF16)


def begin_kernel(first, heads, *refs):
    if first:
        (x, xh, w1, filt, gain, keep, segoff, prevoff, pr) = refs[:9]
        (nx, nh, pre, xin, val, vst, bm, cm, cols, rows, msg, raws) = refs[9:]
    else:
        (x, xh, w1, filt, keep, segoff, prevoff, pr) = refs[:8]
        (pre, xin, val, vst, bm, cm, cols, rows, msg, raws) = refs[8:]
    length = x.shape[0]
    wx = heads * HEADDIM
    ch = wx + 2 * STATE
    tiles = length // T

    def norm(block):
        value = block.astype(F32)
        scale = lax.rsqrt(jnp.mean(value * value, axis=-1, keepdims=True) + EPS)
        return (value * scale * gain[...]).astype(BF16)

    if first:
        halo = norm(xh[...])
        nh[...] = halo
    else:
        halo = xh[...]
    projected = mm(halo, w1[:, :ch]).astype(BF16).astype(F32)
    xin[0:8, :] = projected[8:16, :]
    for i in range(tiles):
        at = slice(T * i, T * i + T)
        if first:
            block = norm(x[at, :])
            nx[at, :] = block
        else:
            block = x[at, :]
        proj = mm(block, w1[:, : ch + 128])
        xin[8 + T * i : 8 + T * i + T, :] = proj[:, :ch].astype(BF16).astype(F32)
        raws[at, :] = proj[:, ch:]
    raw = jnp.transpose(raws[...])[0:8, :]
    z = raw + pr[0:8, 0:1]
    sig = sigmoid(z)
    steps = jnp.maximum(z, 0.0) + jnp.log1p(jnp.exp(-jnp.abs(z)))
    a = steps * pr[8:16, 0:1]
    tri = (
        lax.broadcasted_iota(jnp.int32, (T, T), 0) <= lax.broadcasted_iota(jnp.int32, (T, T), 1)
    ).astype(F32)
    carry = jnp.zeros((8, 1), F32)
    parts = []
    for i in range(tiles):
        part = (
            lax.dot_general(
                a[:, T * i : T * i + T],
                tri,
                (((1,), (0,)), ((), ())),
                precision=HIGHEST,
                preferred_element_type=F32,
            )
            + carry
        )
        parts.append(part)
        carry = part[:, T - 1 : T]
    logs = jnp.concatenate(parts, axis=1) - segoff[...]
    end = logs[:, length - 1 : length]
    into = jnp.exp(logs + prevoff[:, 0:1])
    tail = jnp.exp(end - logs)
    through = jnp.exp(end + prevoff[:, 0:1])
    everything = jnp.concatenate([logs, steps, into, tail], axis=0)
    rows[0:32, :] = everything
    rows[32:40, :] = sig
    cols[...] = to_cols(everything)
    state = jnp.zeros((wx, STATE), F32)
    for i in range(tiles):
        at = slice(T * i, T * i + T)
        total = filt[4:5, :] + filt[3:4, :] * xin[8 + T * i : 8 + T * i + T, :]
        for k in range(1, KCONV):
            moved = xin[8 + T * i - k : 8 + T * i - k + T, :]
            total = total + filt[3 - k : 4 - k, :] * moved * keep[at, k : k + 1]
        pre[at, :] = total
        act = total * sigmoid(total)
        col = cols[at, :]
        v = act[:, :wx]
        val[at, :] = v
        stepped = v * spread(col, 8, heads)
        vst[at, :] = stepped.astype(BF16)
        bt = act[:, wx : wx + STATE].astype(BF16)
        bm[at, :] = bt
        cm[at, :] = act[:, wx + STATE : ch].astype(BF16)
        state = state + mm_tn((stepped * spread(col, 24, heads)).astype(BF16), bt)
    pack_message(msg, state, through, wx)


def split_heads(vst, q, n):
    block = vst[0:n, 128 * q : 128 * q + 128]
    low = lax.broadcasted_iota(jnp.int32, (n, 128), 1) < HEADDIM
    zero = jnp.zeros_like(block)
    return jnp.where(low, block, zero), jnp.where(low, zero, block)


def decay_tile(cols, rows, h, i, n):
    gap = cols[:, h : h + 1] - rows[h : h + 1, 0:n]
    e = jnp.exp(gap)
    allowed = (
        lax.broadcasted_iota(jnp.int32, (T, n), 0) + T * i
        >= lax.broadcasted_iota(jnp.int32, (T, n), 1)
    )
    return jnp.where(allowed, e, 0.0)


def inner_kernel(heads, vst, bm, cm, cols, rows, yloc):
    length = vst.shape[0]
    for i in range(length // T):
        n = T * (i + 1)
        at = slice(T * i, T * i + T)
        scores = mm_nt(cm[at, :], bm[0:n, :])
        col = cols[at, :]
        for q in range(heads // 2):
            mixes = []
            for h in (2 * q, 2 * q + 1):
                mixes.append((decay_tile(col, rows, h, i, n) * scores).astype(BF16))
            low, high = split_heads(vst, q, n)
            yloc[at, 128 * q : 128 * q + 128] = mm(mixes[0], low) + mm(mixes[1], high)


def finish_kernel(heads, count, nback, *refs):
    idx = refs[0]
    msgs = refs[1 : 1 + nback]
    (nx, w2, yloc, cm, val, cols, hrow, y, gate, sin) = refs[1 + nback : 11 + nback]
    outs = refs[11 + nback :]
    wx = heads * HEADDIM
    state = joined([m[...] for m in msgs], heads)
    sb = state.astype(BF16)
    sin[...] = sb
    j = idx[0]
    for d in range(count):
        at = pl.ds(pl.multiple_of((j ^ d) * T, T), T)
        col = cols[at, :]
        from_state = mm_nt(cm[at, :], sb) * spread(col, 16, heads)
        yt = yloc[at, :] + from_state + hrow[1:2, :] * val[at, :]
        y[at, :] = yt
        g = mm(nx[at, :], w2[:, :wx]).astype(BF16)
        gate[at, :] = g
        gf = g.astype(F32)
        mixed = yt * (gf * sigmoid(gf))
        squares = jnp.sum(mixed * mixed, axis=-1, keepdims=True)
        high = squares.astype(BF16).astype(F32)
        lane = lax.broadcasted_iota(jnp.int32, (T, 128), 1)
        extra = jnp.where(lane == 0, high, jnp.where(lane == 1, squares - high, 0.0))
        outs[d][:, :D] = mm_nt((mixed * hrow[0:1, :]).astype(BF16), w2[:, wx:]).astype(BF16)
        outs[d][:, D:] = extra.astype(BF16)


def write_grad(out, grad, u, scale):
    gb = grad.astype(BF16)
    out[:, :D] = gb
    cross = jnp.sum(gb.astype(F32) * u, axis=-1, keepdims=True)
    k = scale * scale * scale * cross / INNER
    sh = scale.astype(BF16).astype(F32)
    kh = k.astype(BF16).astype(F32)
    lane = lax.broadcasted_iota(jnp.int32, (grad.shape[0], 128), 1)
    extra = jnp.where(
        lane == 0,
        sh,
        jnp.where(lane == 1, scale - sh, jnp.where(lane == 2, kh, jnp.where(lane == 3, k - kh, 0.0))),
    )
    out[:, D:] = extra.astype(BF16)


def owner_forward(last, count, *refs):
    parts = refs[:count]
    hidden, other, newh, out, uo, so = refs[count:]
    total = parts[0][...].astype(F32)
    for part in parts[1:]:
        total = total + part[...].astype(F32)
    u = total[:, :D]
    squares = total[:, D : D + 1] + total[:, D + 1 : D + 2]
    scale = lax.rsqrt(squares / INNER + EPS)
    value = hidden[...].astype(F32) + scale * u
    newh[...] = value
    uo[...] = u
    so[...] = jnp.broadcast_to(scale, so.shape)
    if last:
        write_grad(out, other[...].astype(F32), u, scale)
    else:
        scale_in = lax.rsqrt(jnp.mean(value * value, axis=-1, keepdims=True) + EPS)
        out[...] = (value * scale_in * other[...]).astype(BF16)


def owner_backward(more, count, *refs):
    parts = refs[:count]
    if more:
        grad, hidden, gain, u, scale, newg, out = refs[count:]
    else:
        grad, hidden, gain, newg = refs[count:]
    total = parts[0][...].astype(F32)
    for part in parts[1:]:
        total = total + part[...].astype(F32)
    h = hidden[...].astype(F32)
    scale_in = lax.rsqrt(jnp.mean(h * h, axis=-1, keepdims=True) + EPS)
    weighted = total * gain[...]
    value = (
        grad[...].astype(F32)
        + scale_in * weighted
        - h * (scale_in * scale_in * scale_in) * jnp.mean(weighted * h, axis=-1, keepdims=True)
    )
    newg[...] = value
    if more:
        write_grad(out, value, u[...], scale[:, 0:1])


def gate_back_kernel(heads, gb, w2, y, gate, val, cm, cols, rows, hrow, gy, ggate, gated, msg, sums):
    length = gb.shape[0]
    wx = heads * HEADDIM
    state = jnp.zeros((wx, STATE), F32)
    gain_sum = jnp.zeros((1, wx), F32)
    skip_sum = jnp.zeros((1, wx), F32)
    gain = hrow[0:1, :]
    for i in range(length // T):
        at = slice(T * i, T * i + T)
        extra = gb[at, D:].astype(F32)
        s = extra[:, 0:1] + extra[:, 1:2]
        k = extra[:, 2:3] + extra[:, 3:4]
        gg = mm(gb[at, :D], w2[:, wx:])
        g = gate[at, :].astype(F32)
        sg = sigmoid(g)
        ga = g * sg
        yt = y[at, :]
        mixed = yt * ga
        ms = mixed * s
        gain_sum = gain_sum + jnp.sum(gg * ms, axis=0, keepdims=True)
        gated[at, :] = (ms * gain).astype(BF16)
        gm = s * (gg * gain) - mixed * k
        gyt = gm * ga
        gy[at, :] = gyt
        ggate[at, :] = (gm * yt * (sg * (1.0 + g * (1.0 - sg)))).astype(BF16)
        skip_sum = skip_sum + jnp.sum(gyt * val[at, :], axis=0, keepdims=True)
        gc = (gyt * spread(cols[at, :], 16, heads)).astype(BF16)
        state = state + mm_tn(gc, cm[at, :])
    through = rows[16:24, length - 1 : length]
    pack_message(msg, state, through, wx)
    sums[0:1, :] = gain_sum
    sums[1:2, :] = skip_sum
    sums[2:8, :] = jnp.zeros((6, wx), F32)


def inner_back_kernel(heads, gy, vst, bm, cm, cols, rows, dvst, db, dc, dlog, rsum):
    length = vst.shape[0]
    dvst[...] = jnp.zeros(dvst.shape, F32)
    db[...] = jnp.zeros(db.shape, F32)
    dlog[...] = jnp.zeros(dlog.shape, F32)
    lane = lax.broadcasted_iota(jnp.int32, (T, 128), 1)
    for i in range(length // T):
        n = T * (i + 1)
        at = slice(T * i, T * i + T)
        ct = cm[at, :]
        scores = mm_nt(ct, bm[0:n, :])
        col = cols[at, :]
        dk = jnp.zeros((T, n), F32)
        acc = jnp.zeros((T, 128), F32)
        for q in range(heads // 2):
            g2 = gy[at, 128 * q : 128 * q + 128].astype(BF16)
            zero = jnp.zeros_like(g2)
            vb = vst[0:n, 128 * q : 128 * q + 128]
            update = None
            for h in (2 * q, 2 * q + 1):
                gh = jnp.where((lane < HEADDIM) == (h % 2 == 0), g2, zero)
                e = decay_tile(col, rows, h, i, n)
                t1 = mm_nt(gh, vb) * e
                dk = dk + t1
                x = t1 * scores
                acc = jnp.where(lane == h, jnp.sum(x, axis=-1, keepdims=True), acc)
                dlog[h : h + 1, 0:n] -= jnp.sum(x, axis=0, keepdims=True)
                term = mm_tn((e * scores).astype(BF16), gh)
                update = term if update is None else update + term
            dvst[0:n, 128 * q : 128 * q + 128] += update
        rsum[at, :] = acc
        dkb = dk.astype(BF16)
        dc[at, :] = mm(dkb, bm[0:n, :])
        db[0:n, :] += mm_tn(dkb, ct)
    dlog[...] += jnp.transpose(rsum[...])[0:8, :]


def chain_back_kernel(heads, nback, *refs):
    msgs = refs[:nback]
    (gy, vst, val, bm, cm, cols, rows, sin, dvst, db, dc, dlog, pre, xin, keep, filt, hrow, sums,
     pr, w1) = refs[nback : nback + 20]
    gpx, gph, gn_halo, small, ds, dm = refs[nback + 20 :]
    length = vst.shape[0]
    wx = heads * HEADDIM
    ch = wx + 2 * STATE
    tiles = length // T
    after = joined([m[...] for m in msgs], heads)
    ab = after.astype(BF16)
    sb = sin[...]
    lane_head = (
        lax.broadcasted_iota(jnp.int32, (wx, 128), 0) // HEADDIM
        == lax.broadcasted_iota(jnp.int32, (wx, 128), 1)
    ).astype(BF16)
    row_head = (
        lax.broadcasted_iota(jnp.int32, (8, wx), 1) // HEADDIM
        == lax.broadcasted_iota(jnp.int32, (8, wx), 0)
    ).astype(F32)
    pad = dm.shape[1] - length
    for k in range(KCONV - 1):
        dm[k, 0:8, :] = jnp.zeros((8, ch), F32)
        dm[k, length + 8 : length + pad, :] = jnp.zeros((pad - 8, ch), F32)
    filt_sums = [jnp.zeros((1, ch), F32) for _ in range(KCONV + 1)]
    plain = dm.shape[0] - 1
    dm[plain, 0:8, :] = jnp.zeros((8, ch), F32)
    dm[plain, length + 8 : length + pad, :] = jnp.zeros((pad - 8, ch), F32)
    for i in range(tiles):
        at = slice(T * i, T * i + T)
        col = cols[at, :]
        gyt = gy[at, :]
        gc = gyt * spread(col, 16, heads)
        gcb = gc.astype(BF16)
        te = spread(col, 24, heads)
        vt = vst[at, :].astype(F32) * te
        vtb = vt.astype(BF16)
        zin = mm_nt(cm[at, :], sb)
        ua = mm_nt(bm[at, :], ab)
        dct = dc[at, :] + mm(gcb, sb)
        dbt = db[at, :] + mm(vtb, ab)
        dv = dvst[at, :] + te * ua
        a1 = mm((gc * zin).astype(BF16), lane_head)
        a2 = mm((vt * ua).astype(BF16), lane_head)
        a3 = mm((val[at, :] * dv).astype(BF16), lane_head)
        ds[0, at, :] = a1 - a2
        ds[1, at, :] = a2
        ds[2, at, :] = a3
        dvt = spread(col, 8, heads) * dv + hrow[1:2, :] * gyt
        p = pre[at, :]
        sg = sigmoid(p)
        slope = sg * (1.0 + p * (1.0 - sg))
        dp = jnp.concatenate([dvt, dbt, dct], axis=1) * slope
        dm[plain, 8 + T * i : 8 + T * i + T, :] = dp
        filt_sums[4] = filt_sums[4] + jnp.sum(dp, axis=0, keepdims=True)
        filt_sums[3] = filt_sums[3] + jnp.sum(
            dp * xin[8 + T * i : 8 + T * i + T, :], axis=0, keepdims=True
        )
        for k in range(1, KCONV):
            dk = dp * keep[at, k : k + 1]
            dm[k - 1, 8 + T * i : 8 + T * i + T, :] = dk
            moved = xin[8 + T * i - k : 8 + T * i - k + T, :]
            filt_sums[3 - k] = filt_sums[3 - k] + jnp.sum(dk * moved, axis=0, keepdims=True)
    total = jnp.zeros((8, ch), F32)
    for k in range(1, KCONV):
        total = total + filt[3 - k : 4 - k, :] * dm[k - 1, k : k + 8, :]
    halo = jnp.concatenate([jnp.zeros((8, ch), F32), total], axis=0).astype(BF16)
    gph[...] = halo
    gn_halo[...] = mm_nt(halo, w1[:, :ch]).astype(BF16)
    for i in range(tiles):
        total = filt[3:4, :] * dm[plain, 8 + T * i : 8 + T * i + T, :]
        for k in range(1, KCONV):
            total = total + filt[3 - k : 4 - k, :] * dm[k - 1, 8 + T * i + k : 8 + T * i + k + T, :]
        gpx[T * i : T * i + T, :ch] = total.astype(BF16)
    d1 = jnp.transpose(ds[0])[0:8, :]
    d2 = jnp.transpose(ds[1])[0:8, :]
    d3 = jnp.transpose(ds[2])[0:8, :]
    through = rows[16:24, length - 1 : length]
    states = lax.dot_general(
        row_head,
        after * sb.astype(F32),
        (((1,), (0,)), ((), ())),
        precision=HIGHEST,
        preferred_element_type=F32,
    )
    at_end = jnp.sum(d2, axis=-1, keepdims=True) + through * jnp.sum(
        states, axis=-1, keepdims=True
    )
    dl = dlog[...] + d1
    tri = (
        lax.broadcasted_iota(jnp.int32, (T, T), 0) >= lax.broadcasted_iota(jnp.int32, (T, T), 1)
    ).astype(F32)
    carry = at_end
    parts = []
    for i in reversed(range(tiles)):
        part = (
            lax.dot_general(
                dl[:, T * i : T * i + T],
                tri,
                (((1,), (0,)), ((), ())),
                precision=HIGHEST,
                preferred_element_type=F32,
            )
            + carry
        )
        parts.append(part)
        carry = part[:, 0:1]
    da = jnp.concatenate(parts[::-1], axis=1)
    rates = pr[8:16, 0:1]
    steps = rows[8:16, :]
    graw = (d3 + da * rates) * rows[32:40, :]
    gpx[:, ch:] = to_cols(graw).astype(BF16)
    bias_sum = jnp.sum(graw, axis=-1, keepdims=True)
    decay_sum = jnp.sum(da * steps, axis=-1, keepdims=True) * rates
    skip_sum = jnp.sum(row_head * sums[1:2, :], axis=-1, keepdims=True)

    def per_lane(v):
        return jnp.concatenate(
            [jnp.sum(row_head * v, axis=0, keepdims=True), jnp.zeros((1, 2 * STATE), F32)], axis=1
        )

    small[...] = jnp.concatenate(
        filt_sums
        + [
            jnp.concatenate([sums[0:1, :], jnp.zeros((1, 2 * STATE), F32)], axis=1),
            per_lane(decay_sum),
            per_lane(bias_sum),
            per_lane(skip_sum),
            jnp.zeros((7, ch), F32),
        ],
        axis=0,
    )


def pull_kernel(heads, count, *refs):
    idx, gpx, ggate, arrived, w1, w2 = refs[:6]
    outs = refs[6:]
    wx = heads * HEADDIM
    length = gpx.shape[0]
    j = idx[0]
    for d in range(count):
        block = j ^ d
        at = pl.ds(pl.multiple_of(block * T, T), T)
        total = mm_nt(gpx[at, :], w1[...]) + mm_nt(ggate[at, :], w2[:, :wx])
        outs[d][0 : T - 16, :] = total[0 : T - 16, :].astype(BF16)
        late = arrived[...].astype(F32) * (block == length // T - 1).astype(F32)
        outs[d][T - 16 :, :] = (total[T - 16 :, :] + late).astype(BF16)


def shifted(block, axis, distance):
    devices = range(lax.axis_size(axis))
    route = [(i - distance, i) for i in devices if i - distance in devices]
    return lax.ppermute(block, axis, route)


def exchanged(block, axis, distance):
    return lax.ppermute(block, axis, [(i, i ^ distance) for i in range(lax.axis_size(axis))])


def per_device(
    stream,
    segment_ids,
    cotangent,
    norm_gain,
    in_weight,
    bc_weight,
    step_weight,
    filter_x,
    filter_bc,
    decay_log,
    step_bias,
    skip_gain,
    gate_gain,
    out_weight,
):
    length = segment_ids.shape[0]
    heads = decay_log.shape[1]
    wx = heads * HEADDIM
    ch = wx + 2 * STATE
    wide = lax.axis_size("wide")
    tp = lax.axis_size("tp")
    rows = stream.shape[0]
    share = D // wide
    hx = HEADDIM // wide
    hb = 2 * STATE // wide
    nback = -(-(SEQ - 1) // length)
    place = lax.axis_index("tp").astype(jnp.int32).reshape(1)

    def small_params(layer):
        fx = jnp.concatenate([filter_x[layer], gate_gain[layer][None]], axis=0)
        fx = jnp.pad(fx, ((0, 0), (0, 7 - heads), (0, 8 - hx))).reshape(KCONV + 2, 56)
        fb = jnp.pad(filter_bc[layer], ((0, 1), (0, 64 - hb)))
        return jnp.pad(jnp.concatenate([fx, fb], axis=1), ((0, share - KCONV - 2), (0, 0)))

    def first_weights(layer):
        tail = jnp.concatenate(
            [
                step_weight[layer],
                jnp.zeros((share, 7 - heads), BF16),
                norm_gain[layer][:, None],
                small_params(layer),
            ],
            axis=1,
        )
        return jnp.concatenate([in_weight[layer, :, 1, :], bc_weight[layer], tail], axis=1)

    def second_weights(layer):
        return jnp.concatenate([in_weight[layer, :, 0, :], out_weight[layer].T], axis=1)

    packed = [
        [lax.all_gather(first_weights(0), "wide", axis=0, tiled=True)],
        [lax.all_gather(second_weights(0), "wide", axis=0, tiled=True)],
    ]
    for layer in range(1, LAYERS):
        packed[0].append(lax.all_gather(first_weights(layer), "wide", axis=0, tiled=True))
        packed[1].append(lax.all_gather(second_weights(layer), "wide", axis=0, tiled=True))

    p_of = lax.broadcasted_iota(jnp.int32, (wide, 128, ch), 0)
    l_of = lax.broadcasted_iota(jnp.int32, (wide, 128, ch), 1)
    c_of = lax.broadcasted_iota(jnp.int32, (wide, 128, ch), 2)
    x_lane = 8 + (c_of // HEADDIM) * 8 + (c_of % HEADDIM) % hx
    x_place = (c_of % HEADDIM) // hx
    b_lane = 64 + (c_of - wx) % hb
    b_place = (c_of - wx) // hb
    lanes = jnp.where(c_of < wx, x_lane, b_lane)
    places = jnp.where(c_of < wx, x_place, b_place)
    select = ((l_of == lanes) & (p_of == places)).astype(BF16)

    def unpacked(layer):
        w1 = packed[0][layer]
        block = w1.reshape(wide, share, D)[:, : KCONV + 2, ch:]
        found = jnp.einsum("prl,plc->rc", block, select, preferred_element_type=F32)
        filt = jnp.pad(found, ((0, 8 - KCONV - 2), (0, 0)))
        gain = w1[:, ch + 7].astype(F32)[None, :]
        skip = jnp.repeat(skip_gain[layer], HEADDIM)[None, :]
        hrow = jnp.concatenate([found[KCONV + 1 :, :wx], skip, jnp.zeros((6, wx), F32)], axis=0)
        return filt, gain, hrow

    seg_before = shifted(segment_ids[length - 8 :], "wide", 1)
    seg_pad = jnp.concatenate([seg_before, segment_ids])
    keep = jnp.stack(
        [(seg_pad[8 - k : 8 - k + length] == segment_ids).astype(F32) for k in range(8)], axis=1
    )
    zero_seg = segment_ids[0]
    segoff = jnp.broadcast_to(((segment_ids - zero_seg).astype(F32) * OFF)[None, :], (8, length))
    prevoff = jnp.broadcast_to((seg_before[7] - zero_seg).astype(F32) * OFF, (8, 128))

    def head_params(layer):
        both = jnp.concatenate([step_bias[layer][None], -jnp.exp(decay_log[layer])[None]], axis=0)
        both = jnp.pad(both, ((0, 0), (0, 8 - heads))).reshape(16, 1)
        return jnp.broadcast_to(both, (16, 128))

    hidden = stream
    incoming = stream
    memos = []
    for layer in range(LAYERS):
        filt, gain, hrow = unpacked(layer)
        w1, w2 = packed[0][layer], packed[1][layer]
        pr = head_params(layer)
        x = lax.all_gather(incoming, "tp", axis=0, tiled=True)
        xh = shifted(x[length - 16 :], "wide", 1)
        outs = [
            ((length, ch), F32),
            ((length + 8, ch), F32),
            ((length, wx), F32),
            ((length, wx), BF16),
            ((length, STATE), BF16),
            ((length, STATE), BF16),
            ((length, 128), F32),
            ((40, length), F32),
            ((wx + 16, STATE), BF16),
        ]
        if layer == 0:
            outs = [((length, D), BF16), ((16, D), BF16)] + outs
            found = call(
                partial(begin_kernel, True, heads), outs, x, xh, w1, filt, gain, keep, segoff,
                prevoff, pr, scratch=[((length, 128), F32)],
            )
            nx, nh = found[:2]
            found = found[2:]
        else:
            nx, nh = x, xh
            found = call(
                partial(begin_kernel, False, heads), outs, x, xh, w1, filt, keep, segoff,
                prevoff, pr, scratch=[((length, 128), F32)],
            )
        pre, xin, val, vst, bm, cm, cols, srows, msg = found
        msgs = [shifted(msg, "wide", d) for d in range(1, nback + 1)]
        (yloc,) = call(
            partial(inner_kernel, heads), [((length, wx), F32)], vst, bm, cm, cols, srows
        )
        found = call(
            partial(finish_kernel, heads, tp, nback),
            [((length, wx), F32), ((length, wx), BF16), ((wx, STATE), BF16)]
            + [((rows, D + 128), BF16)] * tp,
            place, *msgs, nx, w2, yloc, cm, val, cols, hrow, smem=1,
        )
        y, gate, sin = found[:3]
        parts = [found[3]] + [exchanged(found[3 + d], "tp", d) for d in range(1, tp)]
        last = layer == LAYERS - 1
        other = cotangent if last else unpacked(layer + 1)[1]
        newh, out, u, scale = call(
            partial(owner_forward, last, tp),
            [
                ((rows, D), F32),
                ((rows, D + 128 if last else D), BF16),
                ((rows, D), F32),
                ((rows, 128), F32),
            ],
            *parts, hidden, other,
        )
        memos.append(
            (hidden, nx, nh, pre, xin, val, vst, bm, cm, cols, srows, y, gate, sin, u, scale, pr,
             filt, gain, hrow)
        )
        hidden = newh
        incoming = out
    result = hidden
    grad = cotangent
    reduced = [None] * LAYERS
    for layer in reversed(range(LAYERS)):
        (old, nx, nh, pre, xin, val, vst, bm, cm, cols, srows, y, gate, sin, u, scale, pr, filt,
         gain, hrow) = memos[layer]
        w1, w2 = packed[0][layer], packed[1][layer]
        gb = lax.all_gather(incoming, "tp", axis=0, tiled=True)
        gy, ggate, gated, msg, sums = call(
            partial(gate_back_kernel, heads),
            [
                ((length, wx), F32),
                ((length, wx), BF16),
                ((length, wx), BF16),
                ((wx + 16, STATE), BF16),
                ((8, wx), F32),
            ],
            gb, w2, y, gate, val, cm, cols, srows, hrow,
        )
        msgs = [shifted(msg, "wide", -d) for d in range(1, nback + 1)]
        dvst, db, dc, dlog = call(
            partial(inner_back_kernel, heads),
            [((length, wx), F32), ((length, STATE), F32), ((length, STATE), F32),
             ((8, length), F32)],
            gy, vst, bm, cm, cols, srows, scratch=[((length, 128), F32)],
        )
        second = jnp.concatenate([mm_tn(nx, ggate), mm_tn(gb[:, :D], gated)], axis=1).astype(BF16)
        gpx, gph, gn_halo, small = call(
            partial(chain_back_kernel, heads, nback),
            [((length, ch + 128), BF16), ((16, ch), BF16), ((16, D), BF16), ((16, ch), F32)],
            *msgs, gy, vst, val, bm, cm, cols, srows, sin, dvst, db, dc, dlog, pre, xin, keep,
            filt, hrow, sums, pr, w1,
            scratch=[((3, length, 128), F32), ((KCONV, length + 16, ch), F32)],
        )
        arrived = shifted(gn_halo, "wide", -1)
        found = call(
            partial(pull_kernel, heads, tp),
            [((rows, D), BF16)] * tp,
            place, gpx, ggate, arrived, w1, w2, smem=1,
        )
        parts = [found[0]] + [exchanged(found[d], "tp", d) for d in range(1, tp)]
        first = mm_tn(nx, gpx) + jnp.pad(mm_tn(nh, gph), ((0, 0), (0, 128)))
        smalls = jnp.einsum(
            "rc,plc->prl", small, select.astype(F32), precision=HIGHEST,
            preferred_element_type=F32,
        )[:, : KCONV + 5]
        smalls = jnp.pad(smalls, ((0, 0), (0, share - KCONV - 5), (ch, 0))).reshape(D, D)
        first = (first + smalls).astype(BF16)
        whole = lax.psum_scatter(
            jnp.concatenate([first, second], axis=1), "wide", scatter_dimension=0, tiled=True
        ).astype(F32)
        reduced[layer] = whole
        if layer > 0:
            before = memos[layer - 1]
            grad, incoming = call(
                partial(owner_backward, True, tp),
                [((rows, D), F32), ((rows, D + 128), BF16)],
                *parts, grad, old, gain, before[14], before[15],
            )
        else:
            (grad,) = call(
                partial(owner_backward, False, tp), [((rows, D), F32)], *parts, grad, old, gain
            )
    both = jnp.stack(reduced, axis=0)
    wg_x = both[:, :, :wx]
    wg_b = both[:, :, wx:ch]
    wg_s = both[:, :, ch : ch + heads]
    wg_g = both[:, :, D : D + wx]
    wg_o = both[:, :, D + wx :]
    in_grad = jnp.stack([wg_g, wg_x], axis=2)
    by_gain = (
        jnp.sum(in_grad * in_weight.astype(F32), axis=(2, 3))
        + jnp.sum(wg_b * bc_weight.astype(F32), axis=2)
        + jnp.sum(wg_s * step_weight.astype(F32), axis=2)
    ) / norm_gain.astype(F32)
    bits = both[:, : KCONV + 5, ch:]
    fx = bits[:, : KCONV + 2, 8 : 8 + 8 * heads].reshape(LAYERS, KCONV + 2, heads, 8)[..., :hx]
    head_sums = bits[:, KCONV + 2 :, 8 : 8 + 8 * heads : 8]
    fb = bits[:, : KCONV + 1, 64 : 64 + hb]
    quarter = share // tp
    to_tp = jnp.concatenate(
        [
            wg_b.reshape(LAYERS, tp, quarter, 2 * STATE).transpose(1, 0, 2, 3).reshape(tp, -1),
            by_gain.reshape(LAYERS, tp, quarter).transpose(1, 0, 2).reshape(tp, -1),
            fb.reshape(LAYERS, KCONV + 1, tp, hb // tp).transpose(2, 0, 1, 3).reshape(tp, -1),
        ],
        axis=1,
    )
    summed = jnp.sum(lax.all_to_all(to_tp, "tp", 0, 0), axis=0)
    n1 = LAYERS * quarter * 2 * STATE
    n2 = n1 + LAYERS * quarter
    return (
        result,
        grad,
        summed[n1:n2].reshape(LAYERS, quarter),
        in_grad,
        summed[:n1].reshape(LAYERS, quarter, 2 * STATE),
        wg_s,
        fx[:, : KCONV + 1],
        summed[n2:].reshape(LAYERS, KCONV + 1, hb // tp),
        head_sums[:, 0],
        head_sums[:, 1],
        head_sums[:, 2],
        fx[:, KCONV + 1],
        jnp.swapaxes(wg_o, 1, 2),
    )


def solution(mesh):
    placed = (
        P(("wide", "tp"), None),
        P("wide"),
        P(("wide", "tp"), None),
        P(None, "wide"),
        P(None, "wide", None, "tp"),
        P(None, "wide", None),
        P(None, "wide", "tp"),
        P(None, None, "tp", "wide"),
        P(None, None, "wide"),
        P(None, "tp"),
        P(None, "tp"),
        P(None, "tp"),
        P(None, "tp", "wide"),
        P(None, "tp", "wide"),
    )
    return jax.shard_map(
        per_device,
        mesh=mesh,
        in_specs=placed,
        out_specs=(
            P(("wide", "tp"), None),
            P(("wide", "tp"), None),
            P(None, ("wide", "tp")),
            P(None, "wide", None, "tp"),
            P(None, ("wide", "tp"), None),
            P(None, "wide", "tp"),
            P(None, None, "tp", "wide"),
            P(None, None, ("wide", "tp")),
            P(None, "tp"),
            P(None, "tp"),
            P(None, "tp"),
            P(None, "tp", "wide"),
            P(None, "tp", "wide"),
        ),
        check_vma=False,
    )
```

```python
from functools import partial

import jax
import jax.numpy as jnp
from jax import lax
from jax.experimental import pallas as pl
from jax.experimental.pallas import tpu as pltpu
from jax.sharding import PartitionSpec as P

D = 768
HEADDIM = 64
STATE = 128
KCONV = 4
SEQ = 1024
LAYERS = 2
INNER = 1536
EPS = 1e-05
OFF = 256.0
T = 128
HIGHEST = lax.Precision.HIGHEST
F32 = jnp.float32
BF16 = jnp.bfloat16


def mm(a, b):
    return lax.dot_general(a, b, (((1,), (0,)), ((), ())), preferred_element_type=F32)


def mm_nt(a, b):
    return lax.dot_general(a, b, (((1,), (1,)), ((), ())), preferred_element_type=F32)


def mm_tn(a, b):
    return lax.dot_general(a, b, (((0,), (0,)), ((), ())), preferred_element_type=F32)


def call(body, outs, *args, scratch=(), smem=0, us=3):
    vm = pl.BlockSpec(memory_space=pltpu.VMEM)
    sm = pl.BlockSpec(memory_space=pltpu.SMEM)
    specs = [sm] * smem + [vm] * (len(args) - smem)
    return pl.pallas_call(
        body,
        out_shape=[jax.ShapeDtypeStruct(s, d) for s, d in outs],
        in_specs=specs,
        out_specs=[vm] * len(outs),
        scratch_shapes=[pltpu.VMEM(s, d) for s, d in scratch],
        compiler_params=pltpu.CompilerParams(vmem_limit_bytes=56 * 1024 * 1024),
        cost_estimate=pl.CostEstimate(
            flops=int(us * 4e8), bytes_accessed=int(us * 3e6), transcendentals=0
        ),
    )(*args)


def sigmoid(v):
    return 1.0 / (1.0 + jnp.exp(-v))


def low_lanes():
    return lax.broadcasted_iota(jnp.int32, (T, 2 * HEADDIM), 1) < HEADDIM


def spread(cols, base, heads):
    low = low_lanes()
    parts = []
    for q in range(heads // 2):
        a = cols[:, base + 2 * q : base + 2 * q + 1]
        b = cols[:, base + 2 * q + 1 : base + 2 * q + 2]
        parts.append(jnp.where(low, a, b))
    return jnp.concatenate(parts, axis=1)


def to_cols(rows):
    pad = jnp.zeros((128 - rows.shape[0], rows.shape[1]), F32)
    return jnp.transpose(jnp.concatenate([rows, pad], axis=0))


def state_rows(message, heads, side):
    top = heads * HEADDIM
    factor = message[top : top + 8, :].astype(F32) + message[top + 8 : top + 16, :].astype(F32)
    if not side:
        return message[:top, :].astype(F32)
    return jnp.concatenate(
        [jnp.broadcast_to(factor[h : h + 1, :], (HEADDIM, STATE)) for h in range(heads)], axis=0
    )


def joined(messages, heads):
    total = state_rows(messages[-1], heads, False)
    for message in messages[-2::-1]:
        total = state_rows(message, heads, False) + state_rows(message, heads, True) * total
    return total


def pack_message(ref, state, through, top):
    ref[:top, :] = state.astype(BF16)
    wide = jnp.broadcast_to(through, (8, STATE))
    high = wide.astype(BF16)
    ref[top:, :] = jnp.concatenate([high.astype(F32), wide - high.astype(F32)], axis=0).astype(BF16)


def begin_kernel(first, heads, *refs):
    if first:
        (x, xh, w1, filt, gain, keep, segoff, prevoff, pr) = refs[:9]
        (nx, nh, pre, xin, val, vst, bm, cm, cols, rows, msg, raws) = refs[9:]
    else:
        (x, xh, w1, filt, keep, segoff, prevoff, pr) = refs[:8]
        (pre, xin, val, vst, bm, cm, cols, rows, msg, raws) = refs[8:]
    length = x.shape[0]
    wx = heads * HEADDIM
    ch = wx + 2 * STATE
    tiles = length // T

    def norm(block):
        value = block.astype(F32)
        scale = lax.rsqrt(jnp.mean(value * value, axis=-1, keepdims=True) + EPS)
        return (value * scale * gain[...]).astype(BF16)

    if first:
        halo = norm(xh[...])
        nh[...] = halo
    else:
        halo = xh[...]
    projected = mm(halo, w1[:, :ch]).astype(BF16).astype(F32)
    xin[0:8, :] = projected[8:16, :]
    for i in range(tiles):
        at = slice(T * i, T * i + T)
        if first:
            block = norm(x[at, :])
            nx[at, :] = block
        else:
            block = x[at, :]
        proj = mm(block, w1[:, : ch + 128])
        xin[8 + T * i : 8 + T * i + T, :] = proj[:, :ch].astype(BF16).astype(F32)
        raws[at, :] = proj[:, ch:]
    raw = jnp.transpose(raws[...])[0:8, :]
    z = raw + pr[0:8, 0:1]
    sig = sigmoid(z)
    steps = jnp.maximum(z, 0.0) + jnp.log1p(jnp.exp(-jnp.abs(z)))
    a = steps * pr[8:16, 0:1]
    tri = (
        lax.broadcasted_iota(jnp.int32, (T, T), 0) <= lax.broadcasted_iota(jnp.int32, (T, T), 1)
    ).astype(F32)
    carry = jnp.zeros((8, 1), F32)
    parts = []
    for i in range(tiles):
        part = (
            lax.dot_general(
                a[:, T * i : T * i + T],
                tri,
                (((1,), (0,)), ((), ())),
                precision=HIGHEST,
                preferred_element_type=F32,
            )
            + carry
        )
        parts.append(part)
        carry = part[:, T - 1 : T]
    logs = jnp.concatenate(parts, axis=1) - segoff[...]
    end = logs[:, length - 1 : length]
    into = jnp.exp(logs + prevoff[:, 0:1])
    tail = jnp.exp(end - logs)
    through = jnp.exp(end + prevoff[:, 0:1])
    everything = jnp.concatenate([logs, steps, into, tail], axis=0)
    rows[0:32, :] = everything
    rows[32:40, :] = sig
    cols[...] = to_cols(everything)
    state = jnp.zeros((wx, STATE), F32)
    for i in range(tiles):
        at = slice(T * i, T * i + T)
        total = filt[4:5, :] + filt[3:4, :] * xin[8 + T * i : 8 + T * i + T, :]
        for k in range(1, KCONV):
            moved = xin[8 + T * i - k : 8 + T * i - k + T, :]
            total = total + filt[3 - k : 4 - k, :] * moved * keep[at, k : k + 1]
        pre[at, :] = total
        act = total * sigmoid(total)
        col = cols[at, :]
        v = act[:, :wx]
        val[at, :] = v
        stepped = v * spread(col, 8, heads)
        vst[at, :] = stepped.astype(BF16)
        bt = act[:, wx : wx + STATE].astype(BF16)
        bm[at, :] = bt
        cm[at, :] = act[:, wx + STATE : ch].astype(BF16)
        state = state + mm_tn((stepped * spread(col, 24, heads)).astype(BF16), bt)
    pack_message(msg, state, through, wx)


def split_heads(vst, q, n):
    block = vst[0:n, 128 * q : 128 * q + 128]
    low = lax.broadcasted_iota(jnp.int32, (n, 128), 1) < HEADDIM
    zero = jnp.zeros_like(block)
    return jnp.where(low, block, zero), jnp.where(low, zero, block)


def decay_tile(cols, rows, h, i, n):
    gap = cols[:, h : h + 1] - rows[h : h + 1, 0:n]
    e = jnp.exp(gap)
    allowed = (
        lax.broadcasted_iota(jnp.int32, (T, n), 0) + T * i
        >= lax.broadcasted_iota(jnp.int32, (T, n), 1)
    )
    return jnp.where(allowed, e, 0.0)


def inner_kernel(heads, vst, bm, cm, cols, rows, yloc):
    length = vst.shape[0]
    for i in range(length // T):
        n = T * (i + 1)
        at = slice(T * i, T * i + T)
        scores = mm_nt(cm[at, :], bm[0:n, :])
        col = cols[at, :]
        for q in range(heads // 2):
            mixes = []
            for h in (2 * q, 2 * q + 1):
                mixes.append((decay_tile(col, rows, h, i, n) * scores).astype(BF16))
            low, high = split_heads(vst, q, n)
            yloc[at, 128 * q : 128 * q + 128] = mm(mixes[0], low) + mm(mixes[1], high)


def finish_kernel(heads, count, nback, *refs):
    idx = refs[0]
    msgs = refs[1 : 1 + nback]
    (nx, w2, yloc, cm, val, cols, hrow, y, gate, sin) = refs[1 + nback : 11 + nback]
    outs = refs[11 + nback :]
    wx = heads * HEADDIM
    state = joined([m[...] for m in msgs], heads)
    sb = state.astype(BF16)
    sin[...] = sb
    j = idx[0]
    for d in range(count):
        at = pl.ds(pl.multiple_of((j ^ d) * T, T), T)
        col = cols[at, :]
        from_state = mm_nt(cm[at, :], sb) * spread(col, 16, heads)
        yt = yloc[at, :] + from_state + hrow[1:2, :] * val[at, :]
        y[at, :] = yt
        g = mm(nx[at, :], w2[:, :wx]).astype(BF16)
        gate[at, :] = g
        gf = g.astype(F32)
        mixed = yt * (gf * sigmoid(gf))
        squares = jnp.sum(mixed * mixed, axis=-1, keepdims=True)
        high = squares.astype(BF16).astype(F32)
        lane = lax.broadcasted_iota(jnp.int32, (T, 128), 1)
        extra = jnp.where(lane == 0, high, jnp.where(lane == 1, squares - high, 0.0))
        outs[d][:, :D] = mm_nt((mixed * hrow[0:1, :]).astype(BF16), w2[:, wx:]).astype(BF16)
        outs[d][:, D:] = extra.astype(BF16)


def write_grad(out, grad, u, scale, joint):
    gb = grad.astype(BF16)
    if joint:
        out[:, :D] = gb
    cross = jnp.sum(gb.astype(F32) * u, axis=-1, keepdims=True)
    k = scale * scale * scale * cross / INNER
    sh = scale.astype(BF16).astype(F32)
    kh = k.astype(BF16).astype(F32)
    lane = lax.broadcasted_iota(jnp.int32, (grad.shape[0], 128), 1)
    extra = jnp.where(
        lane == 0,
        sh,
        jnp.where(lane == 1, scale - sh, jnp.where(lane == 2, kh, jnp.where(lane == 3, k - kh, 0.0))),
    )
    out[:, out.shape[1] - 128 :] = extra.astype(BF16)


def owner_forward(last, count, *refs):
    parts = refs[:count]
    hidden, other, newh, out, uo, so = refs[count:]
    total = parts[0][...].astype(F32)
    for part in parts[1:]:
        total = total + part[...].astype(F32)
    u = total[:, :D]
    squares = total[:, D : D + 1] + total[:, D + 1 : D + 2]
    scale = lax.rsqrt(squares / INNER + EPS)
    value = hidden[...].astype(F32) + scale * u
    newh[...] = value
    uo[...] = u
    so[...] = jnp.broadcast_to(scale, so.shape)
    if last:
        write_grad(out, other[...].astype(F32), u, scale, False)
    else:
        scale_in = lax.rsqrt(jnp.mean(value * value, axis=-1, keepdims=True) + EPS)
        out[...] = (value * scale_in * other[...]).astype(BF16)


def owner_backward(more, count, *refs):
    parts = refs[:count]
    if more:
        grad, hidden, gain, u, scale, newg, out = refs[count:]
    else:
        grad, hidden, gain, newg = refs[count:]
    total = parts[0][...].astype(F32)
    for part in parts[1:]:
        total = total + part[...].astype(F32)
    h = hidden[...].astype(F32)
    scale_in = lax.rsqrt(jnp.mean(h * h, axis=-1, keepdims=True) + EPS)
    weighted = total * gain[...]
    value = (
        grad[...].astype(F32)
        + scale_in * weighted
        - h * (scale_in * scale_in * scale_in) * jnp.mean(weighted * h, axis=-1, keepdims=True)
    )
    newg[...] = value
    if more:
        write_grad(out, value, u[...], scale[:, 0:1], True)


def gate_back_kernel(heads, gb, ex, w2, y, gate, val, cm, cols, rows, hrow, gy, ggate, gated, msg, sums):
    length = gb.shape[0]
    wx = heads * HEADDIM
    state = jnp.zeros((wx, STATE), F32)
    gain_sum = jnp.zeros((1, wx), F32)
    skip_sum = jnp.zeros((1, wx), F32)
    gain = hrow[0:1, :]
    for i in range(length // T):
        at = slice(T * i, T * i + T)
        extra = ex[at, ex.shape[1] - 128 :].astype(F32)
        s = extra[:, 0:1] + extra[:, 1:2]
        k = extra[:, 2:3] + extra[:, 3:4]
        gg = mm(gb[at, :D], w2[:, wx:])
        g = gate[at, :].astype(F32)
        sg = sigmoid(g)
        ga = g * sg
        yt = y[at, :]
        mixed = yt * ga
        ms = mixed * s
        gain_sum = gain_sum + jnp.sum(gg * ms, axis=0, keepdims=True)
        gated[at, :] = (ms * gain).astype(BF16)
        gm = s * (gg * gain) - mixed * k
        gyt = gm * ga
        gy[at, :] = gyt
        ggate[at, :] = (gm * yt * (sg * (1.0 + g * (1.0 - sg)))).astype(BF16)
        skip_sum = skip_sum + jnp.sum(gyt * val[at, :], axis=0, keepdims=True)
        gc = (gyt * spread(cols[at, :], 16, heads)).astype(BF16)
        state = state + mm_tn(gc, cm[at, :])
    through = rows[16:24, length - 1 : length]
    pack_message(msg, state, through, wx)
    sums[0:1, :] = gain_sum
    sums[1:2, :] = skip_sum
    sums[2:8, :] = jnp.zeros((6, wx), F32)


def inner_back_kernel(heads, gy, vst, bm, cm, cols, rows, dvst, db, dc, dlog, rsum):
    length = vst.shape[0]
    dvst[...] = jnp.zeros(dvst.shape, F32)
    db[...] = jnp.zeros(db.shape, F32)
    dlog[...] = jnp.zeros(dlog.shape, F32)
    lane = lax.broadcasted_iota(jnp.int32, (T, 128), 1)
    for i in range(length // T):
        n = T * (i + 1)
        at = slice(T * i, T * i + T)
        ct = cm[at, :]
        scores = mm_nt(ct, bm[0:n, :])
        col = cols[at, :]
        dk = jnp.zeros((T, n), F32)
        acc = jnp.zeros((T, 128), F32)
        for q in range(heads // 2):
            g2 = gy[at, 128 * q : 128 * q + 128].astype(BF16)
            zero = jnp.zeros_like(g2)
            vb = vst[0:n, 128 * q : 128 * q + 128]
            update = None
            for h in (2 * q, 2 * q + 1):
                gh = jnp.where((lane < HEADDIM) == (h % 2 == 0), g2, zero)
                e = decay_tile(col, rows, h, i, n)
                t1 = mm_nt(gh, vb) * e
                dk = dk + t1
                x = t1 * scores
                acc = jnp.where(lane == h, jnp.sum(x, axis=-1, keepdims=True), acc)
                dlog[h : h + 1, 0:n] -= jnp.sum(x, axis=0, keepdims=True)
                term = mm_tn((e * scores).astype(BF16), gh)
                update = term if update is None else update + term
            dvst[0:n, 128 * q : 128 * q + 128] += update
        rsum[at, :] = acc
        dkb = dk.astype(BF16)
        dc[at, :] = mm(dkb, bm[0:n, :])
        db[0:n, :] += mm_tn(dkb, ct)
    dlog[...] += jnp.transpose(rsum[...])[0:8, :]


def chain_tile(i, heads, ab, sb, gy, vst, val, bm, cm, cols, dvst, db, dc, pre, hrow, ds):
    wx = heads * HEADDIM
    lane_head = (
        lax.broadcasted_iota(jnp.int32, (wx, 128), 0) // HEADDIM
        == lax.broadcasted_iota(jnp.int32, (wx, 128), 1)
    ).astype(BF16)
    at = slice(T * i, T * i + T)
    col = cols[at, :]
    gyt = gy[at, :]
    gc = gyt * spread(col, 16, heads)
    te = spread(col, 24, heads)
    vt = vst[at, :].astype(F32) * te
    zin = mm_nt(cm[at, :], sb)
    ua = mm_nt(bm[at, :], ab)
    dct = dc[at, :] + mm(gc.astype(BF16), sb)
    dbt = db[at, :] + mm(vt.astype(BF16), ab)
    dv = dvst[at, :] + te * ua
    a2 = mm((vt * ua).astype(BF16), lane_head)
    ds[0, at, :] = mm((gc * zin).astype(BF16), lane_head) - a2
    ds[1, at, :] = a2
    ds[2, at, :] = mm((val[at, :] * dv).astype(BF16), lane_head)
    dvt = spread(col, 8, heads) * dv + hrow[1:2, :] * gyt
    p = pre[at, :]
    sg = sigmoid(p)
    slope = sg * (1.0 + p * (1.0 - sg))
    return jnp.concatenate([dvt, dbt, dct], axis=1) * slope


def chain_head_kernel(heads, nback, *refs):
    msgs = refs[:nback]
    (gy, vst, val, bm, cm, cols, sin, dvst, db, dc, pre, keep, filt, hrow, w1) = refs[
        nback : nback + 15
    ]
    after, gph, gn_halo, dp0, ds0, hd = refs[nback + 15 :]
    ch = pre.shape[1]
    state = joined([m[...] for m in msgs], heads)
    after[...] = state
    dp = chain_tile(
        0, heads, state.astype(BF16), sin[...], gy, vst, val, bm, cm, cols, dvst, db, dc, pre,
        hrow, ds0,
    )
    dp0[...] = dp
    for k in range(1, KCONV):
        hd[k - 1, 0:8, :] = jnp.zeros((8, ch), F32)
        hd[k - 1, 8:24, :] = dp[0:16, :] * keep[0:16, k : k + 1]
    total = jnp.zeros((8, ch), F32)
    for k in range(1, KCONV):
        total = total + filt[3 - k : 4 - k, :] * hd[k - 1, k : k + 8, :]
    halo = jnp.concatenate([jnp.zeros((8, ch), F32), total], axis=0).astype(BF16)
    gph[...] = halo
    gn_halo[...] = mm_nt(halo, w1[:, :ch]).astype(BF16)


def chain_back_kernel(heads, *refs):
    (gy, vst, val, bm, cm, cols, rows, sin, dvst, db, dc, dlog, pre, xin, keep, filt, hrow, sums,
     pr, after, dp0, ds0, gpx, small, ds, dm) = refs
    length = vst.shape[0]
    wx = heads * HEADDIM
    ch = wx + 2 * STATE
    tiles = length // T
    state = after[...]
    ab = state.astype(BF16)
    sb = sin[...]
    row_head = (
        lax.broadcasted_iota(jnp.int32, (8, wx), 1) // HEADDIM
        == lax.broadcasted_iota(jnp.int32, (8, wx), 0)
    ).astype(F32)
    pad = dm.shape[1] - length
    plain = dm.shape[0] - 1
    for k in range(KCONV):
        dm[k, length + 8 : length + pad, :] = jnp.zeros((pad - 8, ch), F32)
    filt_sums = [jnp.zeros((1, ch), F32) for _ in range(KCONV + 1)]
    for i in range(tiles):
        at = slice(T * i, T * i + T)
        if i == 0:
            dp = dp0[...]
            ds[:, at, :] = ds0[...]
        else:
            dp = chain_tile(
                i, heads, ab, sb, gy, vst, val, bm, cm, cols, dvst, db, dc, pre, hrow, ds
            )
        dm[plain, 8 + T * i : 8 + T * i + T, :] = dp
        filt_sums[4] = filt_sums[4] + jnp.sum(dp, axis=0, keepdims=True)
        filt_sums[3] = filt_sums[3] + jnp.sum(
            dp * xin[8 + T * i : 8 + T * i + T, :], axis=0, keepdims=True
        )
        for k in range(1, KCONV):
            dk = dp * keep[at, k : k + 1]
            dm[k - 1, 8 + T * i : 8 + T * i + T, :] = dk
            moved = xin[8 + T * i - k : 8 + T * i - k + T, :]
            filt_sums[3 - k] = filt_sums[3 - k] + jnp.sum(dk * moved, axis=0, keepdims=True)
    for i in range(tiles):
        total = filt[3:4, :] * dm[plain, 8 + T * i : 8 + T * i + T, :]
        for k in range(1, KCONV):
            total = total + filt[3 - k : 4 - k, :] * dm[k - 1, 8 + T * i + k : 8 + T * i + k + T, :]
        gpx[T * i : T * i + T, :ch] = total.astype(BF16)
    d1 = jnp.transpose(ds[0])[0:8, :]
    d2 = jnp.transpose(ds[1])[0:8, :]
    d3 = jnp.transpose(ds[2])[0:8, :]
    through = rows[16:24, length - 1 : length]
    states = lax.dot_general(
        row_head,
        state * sb.astype(F32),
        (((1,), (0,)), ((), ())),
        precision=HIGHEST,
        preferred_element_type=F32,
    )
    at_end = jnp.sum(d2, axis=-1, keepdims=True) + through * jnp.sum(
        states, axis=-1, keepdims=True
    )
    dl = dlog[...] + d1
    tri = (
        lax.broadcasted_iota(jnp.int32, (T, T), 0) >= lax.broadcasted_iota(jnp.int32, (T, T), 1)
    ).astype(F32)
    carry = at_end
    parts = []
    for i in reversed(range(tiles)):
        part = (
            lax.dot_general(
                dl[:, T * i : T * i + T],
                tri,
                (((1,), (0,)), ((), ())),
                precision=HIGHEST,
                preferred_element_type=F32,
            )
            + carry
        )
        parts.append(part)
        carry = part[:, 0:1]
    da = jnp.concatenate(parts[::-1], axis=1)
    rates = pr[8:16, 0:1]
    steps = rows[8:16, :]
    graw = (d3 + da * rates) * rows[32:40, :]
    gpx[:, ch:] = to_cols(graw).astype(BF16)
    bias_sum = jnp.sum(graw, axis=-1, keepdims=True)
    decay_sum = jnp.sum(da * steps, axis=-1, keepdims=True) * rates
    skip_sum = jnp.sum(row_head * sums[1:2, :], axis=-1, keepdims=True)

    def per_lane(v):
        return jnp.concatenate(
            [jnp.sum(row_head * v, axis=0, keepdims=True), jnp.zeros((1, 2 * STATE), F32)], axis=1
        )

    small[...] = jnp.concatenate(
        filt_sums
        + [
            jnp.concatenate([sums[0:1, :], jnp.zeros((1, 2 * STATE), F32)], axis=1),
            per_lane(decay_sum),
            per_lane(bias_sum),
            per_lane(skip_sum),
            jnp.zeros((7, ch), F32),
        ],
        axis=0,
    )


def pull_kernel(heads, count, *refs):
    idx, gpx, ggate, arrived, w1, w2 = refs[:6]
    outs = refs[6:]
    wx = heads * HEADDIM
    length = gpx.shape[0]
    j = idx[0]
    for d in range(count):
        block = j ^ d
        at = pl.ds(pl.multiple_of(block * T, T), T)
        total = mm_nt(gpx[at, :], w1[...]) + mm_nt(ggate[at, :], w2[:, :wx])
        outs[d][0 : T - 16, :] = total[0 : T - 16, :].astype(BF16)
        late = arrived[...].astype(F32) * (block == length // T - 1).astype(F32)
        outs[d][T - 16 :, :] = (total[T - 16 :, :] + late).astype(BF16)


def gather_kernel(count, *refs):
    idx, blocks, out = refs[0], refs[1:-1], refs[-1]
    share = blocks[0].shape[0]
    for d in range(count):
        at = pl.multiple_of((idx[0] ^ d) * share, 32)
        out[pl.ds(at, share), :] = blocks[d][...]


def scatter_kernel(count, small, *refs):
    if small:
        idx, whole, extra = refs[:3]
        outs = refs[3:]
    else:
        idx, whole = refs[:2]
        outs = refs[2:]
    share = outs[0].shape[0]
    width = whole.shape[1]
    for d in range(count):
        peer = idx[0] ^ d
        at = pl.multiple_of(peer * share, 32)
        block = whole[pl.ds(at, share), :].astype(F32)
        if small:
            top = jnp.concatenate(
                [block[0:16, : width - 128], block[0:16, width - 128 :] + extra[peer]], axis=1
            )
            outs[d][0:16, :] = top.astype(BF16)
            outs[d][16:, :] = block[16:, :].astype(BF16)
        else:
            outs[d][...] = block.astype(BF16)


def weights_kernel(heads, tp, layers, *refs):
    idx = refs[0]
    groups = []
    at = 1
    for count in layers:
        groups.append(refs[at : at + count])
        at += count
    own = refs[at : at + len(layers)]
    at += len(layers)
    ins, outw, steps, bits = refs[at : at + 4]
    tail = refs[at + 4 : at + 4 + tp]
    box = refs[-1]
    wx = heads * HEADDIM
    ch = wx + 2 * STATE
    share = ins.shape[2]
    quarter = share // tp
    for half in range(len(layers)):
        layer, second = half // 2, half % 2
        total = groups[half][0][...].astype(F32)
        for block in groups[half][1:]:
            total = total + block[...].astype(F32)
        weights = own[half][...].astype(F32)
        if second:
            ins[layer, 0] = total[:, :wx]
            padded = jnp.concatenate([total[:, wx:], jnp.zeros((128 - share, wx), F32)], axis=0)
            outw[layer] = jnp.transpose(padded)[:, :share]
            by_gain = by_gain + jnp.sum(total[:, :wx] * weights[:, :wx], axis=-1, keepdims=True)
            by_gain = by_gain / gain
            lane = lax.broadcasted_iota(jnp.int32, (share, 128), 1)
            box[layer, :, 2 * STATE :] = jnp.where(lane == 0, by_gain, 0.0)
            for j in range(tp):
                part = quarter // 1
                box[layer, part * j : part * j + 8, 2 * STATE + 64 : 2 * STATE + 96] = bc_bits
        else:
            ins[layer, 1] = total[:, :wx]
            box[layer, :, : 2 * STATE] = total[:, wx:ch]
            steps[layer] = total[:, ch:]
            bits[layer] = total[0:16, ch:]
            bc_bits = total[0:8, ch + 64 : ch + 96]
            lane = lax.broadcasted_iota(jnp.int32, (share, D), 1)
            by_gain = jnp.sum(
                jnp.where(lane < ch + heads, total * weights, 0.0), axis=-1, keepdims=True
            )
            gain = weights[:, ch + 7 : ch + 8]
    for d in range(tp):
        at = pl.multiple_of((idx[0] ^ d) * quarter, 8)
        for layer in range(len(layers) // 2):
            tail[d][layer] = box[layer, pl.ds(at, quarter), :]


def tail_kernel(*refs):
    parts, out = refs[:-1], refs[-1]
    total = parts[0][...]
    for part in parts[1:]:
        total = total + part[...]
    out[...] = total


def shifted(block, axis, distance):
    devices = range(lax.axis_size(axis))
    route = [(i - distance, i) for i in devices if i - distance in devices]
    return lax.ppermute(block, axis, route)


def exchanged(block, axis, distance):
    return lax.ppermute(block, axis, [(i, i ^ distance) for i in range(lax.axis_size(axis))])


def per_device(
    stream,
    segment_ids,
    cotangent,
    norm_gain,
    in_weight,
    bc_weight,
    step_weight,
    filter_x,
    filter_bc,
    decay_log,
    step_bias,
    skip_gain,
    gate_gain,
    out_weight,
):
    length = segment_ids.shape[0]
    heads = decay_log.shape[1]
    wx = heads * HEADDIM
    ch = wx + 2 * STATE
    wide = lax.axis_size("wide")
    tp = lax.axis_size("tp")
    rows = stream.shape[0]
    share = D // wide
    hx = HEADDIM // wide
    hb = 2 * STATE // wide
    nback = -(-(SEQ - 1) // length)
    place = lax.axis_index("tp").astype(jnp.int32).reshape(1)
    piece = lax.axis_index("wide").astype(jnp.int32).reshape(1)
    direct = wide <= 8

    def small_params(layer):
        fx = jnp.concatenate([filter_x[layer], gate_gain[layer][None]], axis=0)
        fx = jnp.pad(fx, ((0, 0), (0, 7 - heads), (0, 8 - hx))).reshape(KCONV + 2, 56)
        fb = jnp.pad(filter_bc[layer], ((0, 1), (0, 64 - hb)))
        return jnp.pad(jnp.concatenate([fx, fb], axis=1), ((0, share - KCONV - 2), (0, 0)))

    def first_weights(layer):
        tail = jnp.concatenate(
            [
                step_weight[layer],
                jnp.zeros((share, 7 - heads), BF16),
                norm_gain[layer][:, None],
                small_params(layer),
            ],
            axis=1,
        )
        return jnp.concatenate([in_weight[layer, :, 1, :], bc_weight[layer], tail], axis=1)

    def second_weights(layer):
        return jnp.concatenate([in_weight[layer, :, 0, :], out_weight[layer].T], axis=1)

    own = [(first_weights(layer), second_weights(layer)) for layer in range(LAYERS)]

    def gathered(block):
        blocks = [block] + [exchanged(block, "wide", d) for d in range(1, wide)]
        return call(
            partial(gather_kernel, wide), [((D, D), BF16)], piece, *blocks, smem=1, us=1
        )[0]

    if direct:
        later = jnp.concatenate([block for pair in own[1:] for block in pair], axis=1)
        later = lax.all_gather(later, "wide", axis=0, tiled=True)
        w1_first = gathered(own[0][0])
        second, w1_first = lax.optimization_barrier((own[0][1], w1_first))
        packed = [[w1_first], [gathered(second)]]
        for layer in range(1, LAYERS):
            packed[0].append(later[:, 2 * D * (layer - 1) : 2 * D * (layer - 1) + D])
            packed[1].append(later[:, 2 * D * (layer - 1) + D : 2 * D * layer])
    else:
        packed = [
            [lax.all_gather(pair[half], "wide", axis=0, tiled=True) for pair in own]
            for half in range(2)
        ]

    p_of = lax.broadcasted_iota(jnp.int32, (wide, 128, ch), 0)
    l_of = lax.broadcasted_iota(jnp.int32, (wide, 128, ch), 1)
    c_of = lax.broadcasted_iota(jnp.int32, (wide, 128, ch), 2)
    x_lane = 8 + (c_of // HEADDIM) * 8 + (c_of % HEADDIM) % hx
    x_place = (c_of % HEADDIM) // hx
    b_lane = 64 + (c_of - wx) % hb
    b_place = (c_of - wx) // hb
    lanes = jnp.where(c_of < wx, x_lane, b_lane)
    places = jnp.where(c_of < wx, x_place, b_place)
    select = ((l_of == lanes) & (p_of == places)).astype(BF16)

    def unpacked(layer):
        w1 = packed[0][layer]
        block = w1.reshape(wide, share, D)[:, : KCONV + 2, ch:]
        found = jnp.einsum("prl,plc->rc", block, select, preferred_element_type=F32)
        filt = jnp.pad(found, ((0, 8 - KCONV - 2), (0, 0)))
        gain = w1[:, ch + 7].astype(F32)[None, :]
        skip = jnp.repeat(skip_gain[layer], HEADDIM)[None, :]
        hrow = jnp.concatenate([found[KCONV + 1 :, :wx], skip, jnp.zeros((6, wx), F32)], axis=0)
        return filt, gain, hrow

    seg_before = shifted(segment_ids[length - 8 :], "wide", 1)
    seg_pad = jnp.concatenate([seg_before, segment_ids])
    keep = jnp.stack(
        [(seg_pad[8 - k : 8 - k + length] == segment_ids).astype(F32) for k in range(8)], axis=1
    )
    zero_seg = segment_ids[0]
    segoff = jnp.broadcast_to(((segment_ids - zero_seg).astype(F32) * OFF)[None, :], (8, length))
    prevoff = jnp.broadcast_to((seg_before[7] - zero_seg).astype(F32) * OFF, (8, 128))

    def head_params(layer):
        both = jnp.concatenate([step_bias[layer][None], -jnp.exp(decay_log[layer])[None]], axis=0)
        both = jnp.pad(both, ((0, 0), (0, 8 - heads))).reshape(16, 1)
        return jnp.broadcast_to(both, (16, 128))

    hidden = stream
    everyone = lax.optimization_barrier(
        (lax.all_gather(stream, "tp", axis=0, tiled=True),
         lax.all_gather(cotangent, "tp", axis=0, tiled=True))
    )
    incoming = None
    memos = []
    for layer in range(LAYERS):
        filt, gain, hrow = unpacked(layer)
        w1, w2 = packed[0][layer], packed[1][layer]
        pr = head_params(layer)
        x = everyone[0] if layer == 0 else lax.all_gather(incoming, "tp", axis=0, tiled=True)
        xh = shifted(x[length - 16 :], "wide", 1)
        outs = [
            ((length, ch), F32),
            ((length + 8, ch), F32),
            ((length, wx), F32),
            ((length, wx), BF16),
            ((length, STATE), BF16),
            ((length, STATE), BF16),
            ((length, 128), F32),
            ((40, length), F32),
            ((wx + 16, STATE), BF16),
        ]
        if layer == 0:
            outs = [((length, D), BF16), ((16, D), BF16)] + outs
            found = call(
                partial(begin_kernel, True, heads), outs, x, xh, w1, filt, gain, keep, segoff,
                prevoff, pr, scratch=[((length, 128), F32)], us=6,
            )
            nx, nh = found[:2]
            found = found[2:]
        else:
            nx, nh = x, xh
            found = call(
                partial(begin_kernel, False, heads), outs, x, xh, w1, filt, keep, segoff,
                prevoff, pr, scratch=[((length, 128), F32)],
            )
        pre, xin, val, vst, bm, cm, cols, srows, msg = found
        msgs = [shifted(msg, "wide", d) for d in range(1, nback + 1)]
        (yloc,) = call(
            partial(inner_kernel, heads), [((length, wx), F32)], vst, bm, cm, cols, srows, us=4
        )
        found = call(
            partial(finish_kernel, heads, tp, nback),
            [((length, wx), F32), ((length, wx), BF16), ((wx, STATE), BF16)]
            + [((rows, D + 128), BF16)] * tp,
            place, *msgs, nx, w2, yloc, cm, val, cols, hrow, smem=1, us=5,
        )
        y, gate, sin = found[:3]
        parts = [found[3]] + [exchanged(found[3 + d], "tp", d) for d in range(1, tp)]
        last = layer == LAYERS - 1
        other = cotangent if last else unpacked(layer + 1)[1]
        newh, out, u, scale = call(
            partial(owner_forward, last, tp),
            [
                ((rows, D), F32),
                ((rows, 128 if last else D), BF16),
                ((rows, D), F32),
                ((rows, 128), F32),
            ],
            *parts, hidden, other,
        )
        memos.append(
            (hidden, nx, nh, pre, xin, val, vst, bm, cm, cols, srows, y, gate, sin, u, scale, pr,
             filt, gain, hrow)
        )
        hidden = newh
        incoming = out
    result = hidden
    grad = cotangent
    reduced = [None] * LAYERS

    def scattered(whole, smalls):
        extra = () if smalls is None else (smalls,)
        return list(
            call(
                partial(scatter_kernel, wide, smalls is not None),
                [((share, D), BF16)] * wide,
                piece, whole, *extra, smem=1, us=2,
            )
        )

    for layer in reversed(range(LAYERS)):
        (old, nx, nh, pre, xin, val, vst, bm, cm, cols, srows, y, gate, sin, u, scale, pr, filt,
         gain, hrow) = memos[layer]
        w1, w2 = packed[0][layer], packed[1][layer]
        extra = lax.all_gather(incoming, "tp", axis=0, tiled=True)
        gb = everyone[1] if layer == LAYERS - 1 else extra
        gy, ggate, gated, msg, sums = call(
            partial(gate_back_kernel, heads),
            [
                ((length, wx), F32),
                ((length, wx), BF16),
                ((length, wx), BF16),
                ((wx + 16, STATE), BF16),
                ((8, wx), F32),
            ],
            gb, extra, w2, y, gate, val, cm, cols, srows, hrow, us=5,
        )
        msgs = [shifted(msg, "wide", -d) for d in range(1, nback + 1)]
        dvst, db, dc, dlog = call(
            partial(inner_back_kernel, heads),
            [((length, wx), F32), ((length, STATE), F32), ((length, STATE), F32),
             ((8, length), F32)],
            gy, vst, bm, cm, cols, srows, scratch=[((length, 128), F32)], us=7,
        )
        second = jnp.concatenate([mm_tn(nx, ggate), mm_tn(gb[:, :D], gated)], axis=1).astype(BF16)
        if direct and layer == 0:
            second_parts = scattered(second, None)
        after, gph, gn_halo, dp0, ds0 = call(
            partial(chain_head_kernel, heads, nback),
            [((wx, STATE), F32), ((16, ch), BF16), ((16, D), BF16), ((T, ch), F32),
             ((3, T, 128), F32)],
            *msgs, gy, vst, val, bm, cm, cols, sin, dvst, db, dc, pre, keep, filt, hrow, w1,
            scratch=[((3, 24, ch), F32)], us=3,
        )
        arrived = shifted(gn_halo, "wide", -1)
        gpx, small = call(
            partial(chain_back_kernel, heads),
            [((length, ch + 128), BF16), ((16, ch), F32)],
            gy, vst, val, bm, cm, cols, srows, sin, dvst, db, dc, dlog, pre, xin, keep,
            filt, hrow, sums, pr, after, dp0, ds0,
            scratch=[((3, length, 128), F32), ((KCONV, length + 16, ch), F32)], us=7,
        )

        def pulled(gpx):
            found = call(
                partial(pull_kernel, heads, tp),
                [((rows, D), BF16)] * tp,
                place, gpx, ggate, arrived, w1, w2, smem=1, us=5,
            )
            return list(found)

        def first_grad(gpx):
            return mm_tn(nx, gpx) + jnp.pad(mm_tn(nh, gph), ((0, 0), (0, 128)))

        smalls = jnp.einsum(
            "rc,plc->prl", small, select.astype(F32), precision=HIGHEST,
            preferred_element_type=F32,
        )
        if direct and layer == 0:
            first_parts = scattered(first_grad(gpx), smalls)
            first_parts, gpx = lax.optimization_barrier((first_parts, gpx))
            found = pulled(gpx)
        else:
            found = pulled(gpx)
            found, gpx = lax.optimization_barrier((found, gpx))
            smalls = jnp.pad(
                smalls[:, : KCONV + 5], ((0, 0), (0, share - KCONV - 5), (ch, 0))
            ).reshape(D, D)
            first = (first_grad(gpx) + smalls).astype(BF16)
            whole = lax.psum_scatter(
                jnp.concatenate([first, second], axis=1), "wide", scatter_dimension=0, tiled=True
            )
            reduced[layer] = whole
        parts = [found[0]] + [exchanged(found[d], "tp", d) for d in range(1, tp)]
        if layer > 0:
            before = memos[layer - 1]
            grad, incoming = call(
                partial(owner_backward, True, tp),
                [((rows, D), F32), ((rows, D + 128), BF16)],
                *parts, grad, old, gain, before[14], before[15],
            )
        else:
            (grad,) = call(
                partial(owner_backward, False, tp), [((rows, D), F32)], *parts, grad, old, gain
            )
    quarter = share // tp
    hq = hb // tp
    if direct:
        layers = []
        groups = []
        for half in (first_parts, second_parts):
            blocks = [half[0]] + [exchanged(half[d], "wide", d) for d in range(1, wide)]
            groups += blocks
            layers.append(wide)
        for layer in range(1, LAYERS):
            groups += [reduced[layer][:, :D], reduced[layer][:, D:]]
            layers += [1, 1]
        found = call(
            partial(weights_kernel, heads, tp, tuple(layers)),
            [
                ((LAYERS, 2, share, wx), F32),
                ((LAYERS, wx, share), F32),
                ((LAYERS, share, 128), F32),
                ((LAYERS, 16, 128), F32),
            ]
            + [((LAYERS, quarter, 2 * STATE + 128), F32)] * tp,
            place, *groups, *[block for pair in own for block in pair],
            scratch=[((LAYERS, share, 2 * STATE + 128), F32)], smem=1, us=3,
        )
        ins, out_grads, step_sums, bits = found[:4]
        tails = [found[4]] + [exchanged(found[4 + d], "tp", d) for d in range(1, tp)]
        (summed,) = call(
            tail_kernel, [((LAYERS, quarter, 2 * STATE + 128), F32)], *tails, us=1
        )
        in_grad = jnp.transpose(ins, (0, 2, 1, 3))
        bc_grad = summed[:, :, : 2 * STATE]
        gain_grad = summed[:, :, 2 * STATE]
        fb = lax.dynamic_slice_in_dim(
            summed[:, : KCONV + 1, 2 * STATE + 64 : 2 * STATE + 64 + hb], place[0] * hq, hq, axis=2
        )
        step_grad = step_sums[:, :, :heads]
    else:
        both = jnp.stack(reduced, axis=0).astype(F32)
        wg_b = both[:, :, wx:ch]
        step_grad = both[:, :, ch : ch + heads]
        in_grad = jnp.stack([both[:, :, D : D + wx], both[:, :, :wx]], axis=2)
        out_grads = jnp.swapaxes(both[:, :, D + wx :], 1, 2)
        by_gain = (
            jnp.sum(in_grad * in_weight.astype(F32), axis=(2, 3))
            + jnp.sum(wg_b * bc_weight.astype(F32), axis=2)
            + jnp.sum(step_grad * step_weight.astype(F32), axis=2)
        ) / norm_gain.astype(F32)
        bits = both[:, : KCONV + 5, ch:]
        to_tp = jnp.concatenate(
            [
                wg_b.reshape(LAYERS, tp, quarter, 2 * STATE).transpose(1, 0, 2, 3).reshape(tp, -1),
                by_gain.reshape(LAYERS, tp, quarter).transpose(1, 0, 2).reshape(tp, -1),
                bits[:, : KCONV + 1, 64 : 64 + hb]
                .reshape(LAYERS, KCONV + 1, tp, hq).transpose(2, 0, 1, 3).reshape(tp, -1),
            ],
            axis=1,
        )
        summed = jnp.sum(lax.all_to_all(to_tp, "tp", 0, 0), axis=0)
        n1 = LAYERS * quarter * 2 * STATE
        n2 = n1 + LAYERS * quarter
        bc_grad = summed[:n1].reshape(LAYERS, quarter, 2 * STATE)
        gain_grad = summed[n1:n2].reshape(LAYERS, quarter)
        fb = summed[n2:].reshape(LAYERS, KCONV + 1, hq)
    fx = bits[:, : KCONV + 2, 8 : 8 + 8 * heads].reshape(LAYERS, KCONV + 2, heads, 8)[..., :hx]
    head_sums = bits[:, KCONV + 2 : KCONV + 5, 8 : 8 + 8 * heads : 8]
    return (
        result,
        grad,
        gain_grad,
        in_grad,
        bc_grad,
        step_grad,
        fx[:, : KCONV + 1],
        fb,
        head_sums[:, 0],
        head_sums[:, 1],
        head_sums[:, 2],
        fx[:, KCONV + 1],
        out_grads,
    )


def solution(mesh):
    placed = (
        P(("wide", "tp"), None),
        P("wide"),
        P(("wide", "tp"), None),
        P(None, "wide"),
        P(None, "wide", None, "tp"),
        P(None, "wide", None),
        P(None, "wide", "tp"),
        P(None, None, "tp", "wide"),
        P(None, None, "wide"),
        P(None, "tp"),
        P(None, "tp"),
        P(None, "tp"),
        P(None, "tp", "wide"),
        P(None, "tp", "wide"),
    )
    return jax.shard_map(
        per_device,
        mesh=mesh,
        in_specs=placed,
        out_specs=(
            P(("wide", "tp"), None),
            P(("wide", "tp"), None),
            P(None, ("wide", "tp")),
            P(None, "wide", None, "tp"),
            P(None, ("wide", "tp"), None),
            P(None, "wide", "tp"),
            P(None, None, "tp", "wide"),
            P(None, None, ("wide", "tp")),
            P(None, "tp"),
            P(None, "tp"),
            P(None, "tp"),
            P(None, "tp", "wide"),
            P(None, "tp", "wide"),
        ),
        check_vma=False,
    )
```
